1024 devices in a mesh: ctx: 128 (over z_lo, y, x), head: 8 (over z_hi, core).
Axes of the slice: x: 8, y: 8, z: 8 (z_hi: 4, z_lo: 2; z = z_hi * 2 + z_lo), core: 2. Of those that a mesh axis runs over, the one named last changes fastest.
Arguments:
- raw_queries: bfloat16 [16384, 4096], P('ctx', 'head'), may hold values from -4.5 to 4.5
- raw_keys: bfloat16 [16384, 4096], P('ctx', 'head'), may hold values from -4.5 to 4.5
- values: bfloat16 [16384, 4096], P('ctx', 'head'), may hold values from -6 to 6
- output_gradient: bfloat16 [16384, 4096], P('ctx', 'head'), may hold values from -16 to 16
- query_gain: float32 [4096], P('head'), may hold values from 0.1 to 1.9
- key_gain: float32 [4096], P('head'), may hold values from 0.1 to 1.9
- head_kind: int32 [32], P('head'), may hold values from 0 to 1, as said below
Outputs:
- query_gradient: bfloat16 [16384, 4096], P('ctx', 'head')
- key_gradient: bfloat16 [16384, 4096], P('ctx', 'head')
- value_gradient: bfloat16 [16384, 4096], P('ctx', 'head')
The draws below stay inside these ranges and needn't reach their ends.
Inputs may be any that keep to these rules, and one draw needn't show every extreme that they name: `head_kind`: 1 marks a strided head and 0 a local one; each aligned group of 4 heads holds exactly one strided head.
All inputs are finite; a program needn't handle non-finite values.
Results may differ from the reference program's by a relative error of at most 0.01.
Values may be sent and summed in bfloat16 or wider, within the bound.
A program may use at most 32 MiB of HBM per device.

```python
import math
import jax
import jax.numpy as jnp
from jax import lax

HEADS = 32
HD = 128
WINDOW = 1024
STRIDE = 1024
TOKENS = 16384
HEADS_DEV = 4


def field_draw(key, role):
    full_width = HEADS * HD
    column_head = jnp.arange(full_width, dtype=jnp.int32) // HD
    fresh = jax.random.fold_in(key, role)
    ramp_power = column_head.astype(jnp.float32) / max(HEADS - 1, 1)
    base = jax.random.normal(jax.random.fold_in(fresh, 1), (TOKENS, full_width), jnp.float32) * (1.7320508 ** ramp_power)[None, :]
    return jnp.clip(base, -4.5, 4.5).astype(jnp.bfloat16)


def draw_raw_queries(key, part):
    return field_draw(key, 1)


def draw_raw_keys(key, part):
    return field_draw(key, 2)


def draw_head_kind(key, part):
    group_count = HEADS // HEADS_DEV
    chosen = jax.random.randint(jax.random.fold_in(key, 5), (group_count,), 0, HEADS_DEV)
    marked = jnp.arange(HEADS_DEV, dtype=jnp.int32)[None, :] == chosen[:, None]
    return marked.astype(jnp.int32).reshape(HEADS)


def shard_levels(own_key, dims, split, smallest, top_value):
    level, own = 1.0, jax.random.fold_in(own_key, 6)
    for dim, shards_of in split:
        steps = jnp.exp(jax.random.uniform(jax.random.fold_in(own, dim), (shards_of,), jnp.float32, smallest / len(split), top_value / len(split)))
        level = level * jnp.repeat(steps, dims[dim] // shards_of).reshape([-1 if axis == dim else 1 for axis in range(len(dims))])
    return level


def bell_draw(key, extent, deviation, bound, pieces=(), held_as=jnp.bfloat16):
    loudness = shard_levels(key, extent, pieces, -0.22, 0.18) if pieces else 1.0
    drawn = jax.random.normal(key, extent, jnp.float32) * deviation * loudness
    return jnp.minimum(jnp.maximum(drawn, -bound), bound).astype(held_as)


def setup_inputs(seed: int = 0) -> dict:
    key_of = jax.random.split(jax.random.key(seed), 8)
    raw_queries = draw_raw_queries(jax.random.fold_in(key_of[7], 71), 0)
    raw_keys = draw_raw_keys(jax.random.fold_in(key_of[7], 71), 0)
    values = bell_draw(key_of[2], (TOKENS, HEADS * HD), 1.0, 6.0, ((0, 128), (1, 8)))
    output_gradient = bell_draw(key_of[3], (TOKENS, HEADS * HD), 4.0, 16.0, ((0, 128), (1, 8)))
    query_gain = jnp.clip(1.0 + 0.18 * jax.random.normal(key_of[4], (HEADS * HD,), jnp.float32), 0.1, 1.9)
    key_gain = jnp.clip(1.0 + 0.18 * jax.random.normal(key_of[5], (HEADS * HD,), jnp.float32), 0.1, 1.9)
    head_kind = draw_head_kind(jax.random.fold_in(key_of[7], 71), 0)
    return {"raw_queries": raw_queries, "raw_keys": raw_keys, "values": values, "output_gradient": output_gradient, "query_gain": query_gain, "key_gain": key_gain, "head_kind": head_kind}


EPSILON = 1e-06
QUERY_BLOCK = 128

def attend(queries, keys, values, out_grads, allowed):
    score_scale = 1.0 / math.sqrt(HD)
    high = lax.Precision.HIGHEST
    query_f = queries.astype(jnp.float32)
    key_f = keys.astype(jnp.float32)
    value_f = values.astype(jnp.float32)
    grad_f = out_grads.astype(jnp.float32)
    scores = jnp.dot(query_f, key_f.T, precision=high) * score_scale
    masked = jnp.where(allowed, scores, -jnp.inf)
    row_max = lax.optimization_barrier(jnp.max(masked, axis=1, keepdims=True))
    log_total = row_max + jnp.log(lax.optimization_barrier(jnp.sum(jnp.exp(masked - row_max), axis=1, keepdims=True)))
    weights = jnp.exp(masked - log_total)
    weights_low = lax.optimization_barrier(weights.astype(jnp.bfloat16)).astype(jnp.float32)
    outputs = jnp.dot(weights_low, value_f, precision=high)
    delta_rows = lax.optimization_barrier(jnp.sum(grad_f * outputs, axis=1, keepdims=True))
    weight_grads = jnp.dot(grad_f, value_f.T, precision=high)
    score_grads = weights * (weight_grads - delta_rows)
    score_low = lax.optimization_barrier(score_grads.astype(jnp.bfloat16)).astype(jnp.float32)
    value_part = jnp.dot(weights_low.T, grad_f, precision=high)
    query_part = jnp.dot(score_low, key_f, precision=high) * score_scale
    key_part = jnp.dot(score_low.T, query_f, precision=high) * score_scale
    return (query_part, key_part, value_part)

def local_head(queries, keys, values, out_grads):
    key_span = WINDOW + QUERY_BLOCK
    pad_keys = jnp.concatenate([jnp.zeros((WINDOW, HD), keys.dtype), keys])
    pad_values = jnp.concatenate([jnp.zeros((WINDOW, HD), values.dtype), values])

    def advance(carried, block_index):
        key_acc, value_acc = carried
        first_row = (block_index * QUERY_BLOCK).astype(jnp.int32)
        block_queries = lax.dynamic_slice_in_dim(queries, first_row, QUERY_BLOCK)
        block_grads = lax.dynamic_slice_in_dim(out_grads, first_row, QUERY_BLOCK)
        near_keys = lax.dynamic_slice_in_dim(pad_keys, first_row, key_span)
        near_values = lax.dynamic_slice_in_dim(pad_values, first_row, key_span)
        query_pos = first_row + jnp.arange(QUERY_BLOCK, dtype=jnp.int32)
        key_pos = first_row - WINDOW + jnp.arange(key_span, dtype=jnp.int32)
        allowed = (key_pos[None, :] <= query_pos[:, None]) & (key_pos[None, :] > query_pos[:, None] - WINDOW) & (key_pos[None, :] >= 0)
        query_part, key_part, value_part = attend(block_queries, near_keys, near_values, block_grads, allowed)
        key_acc = lax.dynamic_update_slice_in_dim(key_acc, lax.dynamic_slice_in_dim(key_acc, first_row, key_span) + key_part, first_row, 0)
        value_acc = lax.dynamic_update_slice_in_dim(value_acc, lax.dynamic_slice_in_dim(value_acc, first_row, key_span) + value_part, first_row, 0)
        return ((key_acc, value_acc), query_part)
    start_acc = jnp.zeros((WINDOW + TOKENS, HD), jnp.float32)
    (key_acc, value_acc), query_parts = lax.scan(advance, (start_acc, start_acc), jnp.arange(TOKENS // QUERY_BLOCK, dtype=jnp.int32))
    return (query_parts.reshape(TOKENS, HD), key_acc[WINDOW:], value_acc[WINDOW:])

def strided_head(queries, keys, values, out_grads):
    class_length = TOKENS // STRIDE

    def classes(array):
        return array.reshape(class_length, STRIDE, HD).transpose(1, 0, 2)

    def unclass(array):
        return array.transpose(1, 0, 2).reshape(TOKENS, HD)
    index_rows = jnp.arange(class_length, dtype=jnp.int32)
    allowed = index_rows[None, :] <= index_rows[:, None]
    query_part, key_part, value_part = jax.vmap(lambda first, second, third, fourth: attend(first, second, third, fourth, allowed))(classes(queries), classes(keys), classes(values), classes(out_grads))
    return (unclass(query_part), unclass(key_part), unclass(value_part))

def per_head(packed):
    queries, keys, values, out_grads, head_type = packed
    return lax.cond(head_type == 1, strided_head, local_head, queries, keys, values, out_grads)

def normalize(raw, gain):
    raw_f = raw.astype(jnp.float32)
    inverse = lax.rsqrt(lax.optimization_barrier(jnp.mean(raw_f * raw_f, axis=1, keepdims=True)) + EPSILON)
    return (raw_f * inverse * gain).astype(jnp.bfloat16)

def reference(raw_queries, raw_keys, values, output_gradient, query_gain, key_gain, head_kind):
    normed_queries = normalize(raw_queries, query_gain)
    normed_keys = normalize(raw_keys, key_gain)

    def by_head(array):
        return array.reshape(TOKENS, HEADS, HD).transpose(1, 0, 2)

    def joined(array):
        return array.transpose(1, 0, 2).reshape(TOKENS, HEADS * HD).astype(jnp.bfloat16)
    query_parts, key_parts, value_parts = lax.map(per_head, (by_head(normed_queries), by_head(normed_keys), by_head(values), by_head(output_gradient), head_kind))
    return (joined(query_parts), joined(key_parts), joined(value_parts))
```

```python
import functools
import math

import jax
import jax.numpy as jnp
from jax import lax
from jax.experimental import pallas as pl
from jax.experimental.pallas import tpu as pltpu
from jax.sharding import PartitionSpec as P

HD = 128
WINDOW = 1024
STRIDE = 1024
EPSILON = 1e-06
NEAR = 3
MESH = pl.DeviceIdType.MESH
SCORE_SCALE = 1.0 / math.sqrt(HD)


def dot_nt(a, b):
    return lax.dot_general(a, b, (((1,), (1,)), ((), ())), preferred_element_type=jnp.float32)


def dot_tn(a, b):
    return lax.dot_general(a, b, (((0,), (0,)), ((), ())), preferred_element_type=jnp.float32)


def dot_nn(a, b):
    return lax.dot_general(a, b, (((1,), (0,)), ((), ())), preferred_element_type=jnp.float32)


def strided_index(kind_ref):
    index = kind_ref[1] + 2 * kind_ref[2] + 3 * kind_ref[3]
    return jnp.full((1, HD), index, jnp.int32)


def split_heads(heads, index):
    near = [jnp.where(index > g, heads[g], heads[g + 1]) for g in range(NEAR)]
    far = heads[NEAR]
    for g in range(NEAR):
        far = jnp.where(index == g, heads[g], far)
    return near, far


def join_heads(near, far, index):
    joined = []
    for h in range(NEAR + 1):
        if h == 0:
            kept = near[0]
            joined.append(jnp.where(index == 0, far, kept))
        elif h == NEAR:
            joined.append(jnp.where(index == h, far, near[h - 1]))
        else:
            joined.append(
                jnp.where(index == h, far, jnp.where(index > h, near[h], near[h - 1]))
            )
    return joined


def heads_of(ref):
    return [ref[:, h * HD : (h + 1) * HD].astype(jnp.float32) for h in range(NEAR + 1)]


def rounded(array):
    return array.astype(jnp.bfloat16).astype(jnp.float32)


def square_row(heads):
    total = heads[0] * heads[0]
    for part in heads[1:]:
        total = total + part * part
    column = jnp.sum(total, axis=1, keepdims=True)
    return jnp.broadcast_to(column, total.shape).T[0:1, :]


def store_near(ref, near, rows):
    for g in range(NEAR):
        ref[0:rows, g * HD : (g + 1) * HD] = near[g].astype(jnp.bfloat16)


def place(coordinate, ctx_count):
    return {"ctx": lax.rem(coordinate + ctx_count, ctx_count)}


def gather_kernel(
    ctx_count, head_total, kind_ref, q_ref, k_ref, v_ref, g_ref, qgain_ref, kgain_ref,
    qs_ref, ks_ref, vs_ref, gs_ref, far_ref,
    sums, far_out, ring_send, ring_recv, norm_send, norm_recv, far_send, far_recv,
):
    rows = q_ref.shape[0]
    reach = WINDOW // rows
    period = STRIDE // rows
    classes = ctx_count // period
    per_peer = rows // classes
    ctx = lax.axis_index("ctx")
    head = lax.axis_index("head")
    column = lax.rem(ctx, period)
    turn = lax.div(ctx, period)

    right = place(ctx + 1, ctx_count)
    left = place(ctx - 1, ctx_count)
    norm_peers = [lax.rem(head + t, head_total) for t in range(1, head_total)]
    far_peers = [lax.rem(turn + t, classes) * period + column for t in range(1, classes)]

    barrier = pltpu.get_barrier_semaphore()
    greeted = [right, left] + [{"head": p} for p in norm_peers] + [{"ctx": p} for p in far_peers]
    for peer in greeted:
        pl.semaphore_signal(barrier, inc=1, device_id=peer, device_id_type=MESH)

    index = strided_index(kind_ref)
    near_v, far_v = split_heads(heads_of(v_ref), index)
    near_g, far_g = split_heads(heads_of(g_ref), index)
    store_near(vs_ref, near_v, rows)
    store_near(gs_ref, near_g, rows)
    q_heads = heads_of(q_ref)
    k_heads = heads_of(k_ref)
    sums[head] = jnp.concatenate(
        [square_row(q_heads), square_row(k_heads), jnp.zeros((6, HD), jnp.float32)], axis=0
    )
    pl.semaphore_wait(barrier, len(greeted))

    def hop(which, ref, step, peer):
        return pltpu.make_async_remote_copy(
            src_ref=ref.at[pl.ds((step - 1) * rows, rows)],
            dst_ref=ref.at[pl.ds(step * rows, rows)],
            send_sem=ring_send.at[which, step - 1],
            recv_sem=ring_recv.at[which, step - 1],
            device_id=peer,
            device_id_type=MESH,
        )

    rings = [(0, vs_ref, right), (1, gs_ref, left), (2, ks_ref, right), (3, qs_ref, left)]
    hops = {
        (which, step): hop(which, ref, step, peer)
        for which, ref, peer in rings
        for step in range(1, reach + 1)
    }
    norm_copies = []
    for t in range(1, head_total):
        copy = pltpu.make_async_remote_copy(
            src_ref=sums.at[head],
            dst_ref=sums.at[head],
            send_sem=norm_send.at[t],
            recv_sem=norm_recv.at[t],
            device_id={"head": norm_peers[t - 1]},
            device_id_type=MESH,
        )
        copy.start()
        norm_copies.append(copy)
    hops[0, 1].start()
    hops[1, 1].start()

    for copy in norm_copies:
        copy.wait_recv()
    total = sums[0]
    for h in range(1, head_total):
        total = total + sums[h]
    inverse = lax.rsqrt(total / (head_total * (NEAR + 1) * HD) + EPSILON)
    q_scale = jnp.broadcast_to(inverse[0:1, :], (rows, rows)).T
    k_scale = jnp.broadcast_to(inverse[1:2, :], (rows, rows)).T
    q_normed = [
        rounded(part * q_scale * qgain_ref[:, h * HD : (h + 1) * HD])
        for h, part in enumerate(q_heads)
    ]
    k_normed = [
        rounded(part * k_scale * kgain_ref[:, h * HD : (h + 1) * HD])
        for h, part in enumerate(k_heads)
    ]
    near_q, far_q = split_heads(q_normed, index)
    near_k, far_k = split_heads(k_normed, index)
    store_near(ks_ref, near_k, rows)
    store_near(qs_ref, near_q, rows)
    packed = jnp.concatenate(
        [part.reshape(classes, per_peer, HD) for part in (far_q, far_k, far_v, far_g)], axis=1
    )
    far_out[...] = packed.astype(jnp.bfloat16)
    hops[2, 1].start()
    hops[3, 1].start()
    far_copies = []
    for t in range(1, classes):
        copy = pltpu.make_async_remote_copy(
            src_ref=far_out.at[lax.rem(turn + t, classes)],
            dst_ref=far_ref.at[turn],
            send_sem=far_send.at[t],
            recv_sem=far_recv.at[t],
            device_id={"ctx": far_peers[t - 1]},
            device_id_type=MESH,
        )
        copy.start()
        far_copies.append(copy)
    far_ref[turn] = far_out[turn]

    for step in range(1, reach + 1):
        for which, _, _ in rings:
            hops[which, step].wait_recv()
            if step < reach:
                hops[which, step + 1].start()
    for copy in far_copies:
        copy.wait_recv()
    for copy in far_copies + norm_copies + list(hops.values()):
        copy.wait_send()


def local_query_kernel(ctx_count, q_ref, k_ref, v_ref, g_ref, far_ref, dq_ref, stats_ref, far_out):
    span = k_ref.shape[0]
    rows = q_ref.shape[0]
    ctx = lax.axis_index("ctx")
    r = lax.broadcasted_iota(jnp.int32, (span, rows), 0)
    i = lax.broadcasted_iota(jnp.int32, (span, rows), 1)
    block = lax.shift_right_logical(r, int(math.log2(rows)))
    gap = i + block * (2 * rows) - r
    allowed = (gap >= 0) & (gap < WINDOW) & (block <= ctx)
    log_rows, delta_rows = [], []
    for h in range(NEAR):
        cut = slice(h * HD, (h + 1) * HD)
        dq, _, _, log_total, delta = attend(
            q_ref[:, cut], k_ref[:, cut], v_ref[:, cut], g_ref[:, cut], allowed, False
        )
        dq_ref[:, cut] = dq.astype(jnp.bfloat16)
        log_rows.append(log_total)
        delta_rows.append(delta)
    stats_ref[...] = jnp.concatenate(
        log_rows + delta_rows + [jnp.zeros((2, rows), jnp.float32)], axis=0
    )
    classes, quad, _ = far_ref.shape
    per_peer = quad // 4
    gathered = far_ref[...].astype(jnp.float32)
    far_q, far_k, far_v, far_g = [
        gathered[:, a * per_peer : (a + 1) * per_peer, :].reshape(rows, HD).astype(jnp.bfloat16)
        for a in range(4)
    ]
    j = lax.broadcasted_iota(jnp.int32, (rows, rows), 0)
    i = lax.broadcasted_iota(jnp.int32, (rows, rows), 1)
    far_allowed = (j <= i) & (((i - j) & (per_peer - 1)) == 0)
    dq, dk, dv, _, _ = attend(far_q, far_k, far_v, far_g, far_allowed, True)
    parts = [part.reshape(classes, per_peer, HD) for part in (dq, dk, dv, jnp.zeros_like(dq))]
    far_out[...] = jnp.concatenate(parts, axis=1).astype(jnp.bfloat16)


def attend(q, k, v, g, allowed, with_keys):
    scores = jnp.where(allowed, dot_nt(k, q) * SCORE_SCALE, -jnp.inf)
    top = jnp.max(scores, axis=0, keepdims=True)
    grown = jnp.exp(scores - top)
    total = jnp.sum(grown, axis=0, keepdims=True)
    weights = grown * (1.0 / total)
    weights_low = weights.astype(jnp.bfloat16)
    weight_grads = dot_nt(v, g)
    delta = jnp.sum(weights_low.astype(jnp.float32) * weight_grads, axis=0, keepdims=True)
    score_low = (weights * (weight_grads - delta)).astype(jnp.bfloat16)
    dq = dot_tn(score_low, k) * SCORE_SCALE
    log_total = top + jnp.log(total)
    if not with_keys:
        return dq, None, None, log_total, delta
    return dq, dot_nn(score_low, q) * SCORE_SCALE, dot_nn(weights_low, g), log_total, delta


def return_kernel(
    ctx_count, stats_ref, far_ref, all_stats, far_back, stat_send, stat_recv, far_send, far_recv
):
    classes = far_ref.shape[0]
    reach = all_stats.shape[0] - 1
    period = ctx_count // classes
    ctx = lax.axis_index("ctx")
    column = lax.rem(ctx, period)
    turn = lax.div(ctx, period)
    far_peers = [lax.rem(turn + t, classes) * period + column for t in range(1, classes)]
    barrier = pltpu.get_barrier_semaphore()
    greeted = [{"ctx": p} for p in far_peers]
    greeted += [place(ctx - o, ctx_count) for o in range(1, reach + 1)]
    greeted += [place(ctx + o, ctx_count) for o in range(1, reach + 1)]
    for peer in greeted:
        pl.semaphore_signal(barrier, inc=1, device_id=peer, device_id_type=MESH)
    all_stats[0] = stats_ref[...]
    far_back[turn] = far_ref[turn]
    pl.semaphore_wait(barrier, len(greeted))
    copies = []
    for t in range(1, classes):
        copies.append(
            pltpu.make_async_remote_copy(
                src_ref=far_ref.at[lax.rem(turn + t, classes)],
                dst_ref=far_back.at[turn],
                send_sem=far_send.at[t],
                recv_sem=far_recv.at[t],
                device_id={"ctx": far_peers[t - 1]},
                device_id_type=MESH,
            )
        )
    for o in range(1, reach + 1):
        copies.append(
            pltpu.make_async_remote_copy(
                src_ref=stats_ref,
                dst_ref=all_stats.at[o],
                send_sem=stat_send.at[o],
                recv_sem=stat_recv.at[o],
                device_id=place(ctx - o, ctx_count),
                device_id_type=MESH,
            )
        )
    for copy in copies:
        copy.start()
    for copy in copies:
        copy.wait_recv()
    for copy in copies:
        copy.wait_send()


def local_key_kernel(
    ctx_count, kind_ref, q_ref, k_ref, v_ref, g_ref, dq_ref, stats_ref, far_ref,
    q_out, k_out, v_out,
):
    rows = k_ref.shape[0]
    blocks = q_ref.shape[0] // rows
    ctx = lax.axis_index("ctx")
    index = strided_index(kind_ref)
    classes, quad, _ = far_ref.shape
    per_peer = quad // 4
    back = far_ref[...].astype(jnp.float32)
    far = [
        back[:, a * per_peer : (a + 1) * per_peer, :].reshape(rows, HD) for a in range(3)
    ]
    j = lax.broadcasted_iota(jnp.int32, (rows, rows), 0)
    i = lax.broadcasted_iota(jnp.int32, (rows, rows), 1)
    near_k, near_v = [], []
    for h in range(NEAR):
        cut = slice(h * HD, (h + 1) * HD)
        k = k_ref[:, cut]
        v = v_ref[:, cut]
        dk = jnp.zeros((rows, HD), jnp.float32)
        dv = jnp.zeros((rows, HD), jnp.float32)
        for o in range(blocks):
            q = q_ref[o * rows : (o + 1) * rows, cut]
            g = g_ref[o * rows : (o + 1) * rows, cut]
            gap = i - j + o * rows
            allowed = (gap >= 0) & (gap < WINDOW) & (i * 0 + (ctx + o) < ctx_count)
            log_row = stats_ref[o, h : h + 1, :]
            delta_row = stats_ref[o, NEAR + h : NEAR + h + 1, :]
            scores = dot_nt(k, q) * SCORE_SCALE
            weights = jnp.where(allowed, jnp.exp(scores - log_row), 0.0)
            score_grads = weights * (dot_nt(v, g) - delta_row)
            dv = dv + dot_nn(weights.astype(jnp.bfloat16), g)
            dk = dk + dot_nn(score_grads.astype(jnp.bfloat16), q)
        near_k.append(dk * SCORE_SCALE)
        near_v.append(dv)
    near_q = [dq_ref[:, h * HD : (h + 1) * HD].astype(jnp.float32) for h in range(NEAR)]
    for out, near, remote in ((q_out, near_q, far[0]), (k_out, near_k, far[1]), (v_out, near_v, far[2])):
        for h, part in enumerate(join_heads(near, remote, index)):
            out[:, h * HD : (h + 1) * HD] = part.astype(jnp.bfloat16)


def on_device(
    ctx_count, head_total, raw_queries, raw_keys, values, output_gradient, query_gain, key_gain, head_kind
):
    rows, width = raw_queries.shape
    reach = WINDOW // rows
    classes = ctx_count // (STRIDE // rows)
    quad = 4 * (rows // classes)
    near_width = NEAR * HD
    low, wide = jnp.bfloat16, jnp.float32
    vmem = pl.BlockSpec(memory_space=pltpu.VMEM)
    smem = pl.BlockSpec(memory_space=pltpu.SMEM)
    dma = pltpu.SemaphoreType.DMA
    span = jax.ShapeDtypeStruct(((reach + 1) * rows, near_width), low)
    far_shape = jax.ShapeDtypeStruct((classes, quad, HD), low)
    all_q, all_k, all_v, all_g, far_in = pl.pallas_call(
        functools.partial(gather_kernel, ctx_count, head_total),
        name="gather",
        out_shape=(span, span, span, span, far_shape),
        in_specs=[smem] + [vmem] * 6,
        out_specs=(vmem,) * 5,
        scratch_shapes=[
            pltpu.VMEM((head_total, 8, HD), wide),
            pltpu.VMEM((classes, quad, HD), low),
            dma((4, reach)),
            dma((4, reach)),
            dma((head_total,)),
            dma((head_total,)),
            dma((classes,)),
            dma((classes,)),
        ],
        compiler_params=pltpu.CompilerParams(collective_id=0, has_side_effects=True),
    )(
        head_kind, raw_queries, raw_keys, values, output_gradient,
        query_gain.reshape(1, width), key_gain.reshape(1, width),
    )
    first = pl.BlockSpec((rows, near_width), lambda s: (0, 0))
    full = pl.BlockSpec(span.shape, lambda s: (0, 0))
    cube = pl.BlockSpec(far_shape.shape, lambda s: (0, 0, 0))
    tile = pl.BlockSpec((8, HD), lambda s: (0, 0))
    near_dq, stats, far_result = pl.pallas_call(
        functools.partial(local_query_kernel, ctx_count),
        name="query_side",
        grid=(1,),
        out_shape=(
            jax.ShapeDtypeStruct((rows, near_width), low),
            jax.ShapeDtypeStruct((8, HD), wide),
            far_shape,
        ),
        in_specs=[first, full, full, first, cube],
        out_specs=(first, tile, cube),
    )(all_q, all_k, all_v, all_g, far_in)
    all_stats, far_back = pl.pallas_call(
        functools.partial(return_kernel, ctx_count),
        name="give_back",
        out_shape=(jax.ShapeDtypeStruct((reach + 1, 8, HD), wide), far_shape),
        in_specs=[vmem] * 2,
        out_specs=(vmem,) * 2,
        scratch_shapes=[dma((reach + 1,)), dma((reach + 1,)), dma((classes,)), dma((classes,))],
        compiler_params=pltpu.CompilerParams(collective_id=1, has_side_effects=True),
    )(stats, far_result)
    result = jax.ShapeDtypeStruct((rows, width), low)
    whole = pl.BlockSpec((rows, width), lambda s: (0, 0))
    return pl.pallas_call(
        functools.partial(local_key_kernel, ctx_count),
        name="key_side",
        grid=(1,),
        out_shape=(result,) * 3,
        in_specs=[
            smem, full, first, first, full, first,
            pl.BlockSpec((reach + 1, 8, HD), lambda s: (0, 0, 0)), cube,
        ],
        out_specs=(whole,) * 3,
    )(head_kind, all_q, all_k, all_v, all_g, near_dq, all_stats, far_back)


def solution(mesh):
    both = P("ctx", "head")
    placed = (both, both, both, both, P("head"), P("head"), P("head"))
    return jax.shard_map(
        functools.partial(on_device, mesh.shape["ctx"], mesh.shape["head"]),
        mesh=mesh,
        in_specs=placed,
        out_specs=(both, both, both),
        check_vma=False,
    )
```

```python
import functools
import math

import jax
import jax.numpy as jnp
from jax import lax
from jax.experimental import pallas as pl
from jax.experimental.pallas import tpu as pltpu
from jax.sharding import PartitionSpec as P

HD = 128
WINDOW = 1024
STRIDE = 1024
EPSILON = 1e-06
NEAR = 3
MESH = pl.DeviceIdType.MESH
SCORE_SCALE = 1.0 / math.sqrt(HD)


def dot_nt(a, b):
    return lax.dot_general(a, b, (((1,), (1,)), ((), ())), preferred_element_type=jnp.float32)


def dot_tn(a, b):
    return lax.dot_general(a, b, (((0,), (0,)), ((), ())), preferred_element_type=jnp.float32)


def dot_nn(a, b):
    return lax.dot_general(a, b, (((1,), (0,)), ((), ())), preferred_element_type=jnp.float32)


def strided_index(kind_ref):
    index = kind_ref[1] + 2 * kind_ref[2] + 3 * kind_ref[3]
    return jnp.full((1, HD), index, jnp.int32)


def split_heads(heads, index):
    near = [jnp.where(index > g, heads[g], heads[g + 1]) for g in range(NEAR)]
    far = heads[NEAR]
    for g in range(NEAR):
        far = jnp.where(index == g, heads[g], far)
    return near, far


def join_heads(near, far, index):
    joined = []
    for h in range(NEAR + 1):
        if h == 0:
            kept = near[0]
            joined.append(jnp.where(index == 0, far, kept))
        elif h == NEAR:
            joined.append(jnp.where(index == h, far, near[h - 1]))
        else:
            joined.append(
                jnp.where(index == h, far, jnp.where(index > h, near[h], near[h - 1]))
            )
    return joined


def heads_of(ref):
    return [ref[:, h * HD : (h + 1) * HD].astype(jnp.float32) for h in range(NEAR + 1)]


def rounded(array):
    return array.astype(jnp.bfloat16).astype(jnp.float32)


def square_row(heads):
    total = heads[0] * heads[0]
    for part in heads[1:]:
        total = total + part * part
    column = jnp.sum(total, axis=1, keepdims=True)
    return jnp.broadcast_to(column, total.shape).T[0:1, :]


def store_near(ref, near, rows):
    for g in range(NEAR):
        ref[0:rows, g * HD : (g + 1) * HD] = near[g].astype(jnp.bfloat16)


def place(coordinate, ctx_count):
    return {"ctx": lax.rem(coordinate + ctx_count, ctx_count)}


def attend(q, k, v, g, allowed):
    scores = jnp.where(allowed, dot_nt(k, q) * SCORE_SCALE, -jnp.inf)
    top = jnp.max(scores, axis=0, keepdims=True)
    grown = jnp.exp(scores - top)
    total = jnp.sum(grown, axis=0, keepdims=True)
    weights = grown * (1.0 / total)
    weights_low = weights.astype(jnp.bfloat16)
    weight_grads = dot_nt(v, g)
    delta = jnp.sum(weights_low.astype(jnp.float32) * weight_grads, axis=0, keepdims=True)
    score_low = (weights * (weight_grads - delta)).astype(jnp.bfloat16)
    dq = dot_tn(score_low, k) * SCORE_SCALE
    return dq, score_low, weights_low, top + jnp.log(total), delta


def backward_kernel(
    ctx_count, head_total, kind_ref, q_ref, k_ref, v_ref, g_ref, qgain_ref, kgain_ref,
    q_out, k_out, v_out,
    qs, ks, vs, gs, sums, stats, far_out, far_in, far_res, far_back, dq_near, dk_near, dv_near,
    ring_send, ring_recv, norm_send, norm_recv, far_send, far_recv, back_send, back_recv,
    stat_send, stat_recv,
):
    rows = q_ref.shape[0]
    reach = WINDOW // rows
    half = reach // 2
    period = STRIDE // rows
    classes = ctx_count // period
    per_peer = rows // classes
    ctx = lax.axis_index("ctx")
    head = lax.axis_index("head")
    column = lax.rem(ctx, period)
    turn = lax.div(ctx, period)
    norm_peers = [{"head": lax.rem(head + t, head_total)} for t in range(1, head_total)]
    far_turns = [lax.rem(turn + t, classes) for t in range(1, classes)]
    far_peers = [{"ctx": t * period + column} for t in far_turns]
    ahead = [place(ctx + o, ctx_count) for o in range(1, reach + 1)]
    behind = [place(ctx - o, ctx_count) for o in range(1, reach + 1)]

    barrier = pltpu.get_barrier_semaphore()
    greeted = ahead + behind + norm_peers + far_peers
    for peer in greeted:
        pl.semaphore_signal(barrier, inc=1, device_id=peer, device_id_type=MESH)

    index = strided_index(kind_ref)
    near_v, far_v = split_heads(heads_of(v_ref), index)
    near_g, far_g = split_heads(heads_of(g_ref), index)
    store_near(vs, near_v, rows)
    store_near(gs, near_g, rows)
    q_heads = heads_of(q_ref)
    k_heads = heads_of(k_ref)
    sums[head] = jnp.concatenate(
        [square_row(q_heads), square_row(k_heads), jnp.zeros((6, HD), jnp.float32)], axis=0
    )
    stats[0] = jnp.zeros((8, HD), jnp.float32)
    pl.semaphore_wait(barrier, len(greeted))

    def remote(src, dst, send_sem, recv_sem, peer):
        return pltpu.make_async_remote_copy(
            src_ref=src, dst_ref=dst, send_sem=send_sem, recv_sem=recv_sem,
            device_id=peer, device_id_type=MESH,
        )

    values, grads, keys, queries = range(4)
    hops = {}
    for which, ref, forward in (
        (values, vs, True), (grads, gs, False), (keys, ks, True), (queries, qs, False)
    ):
        onward, backward = (ahead, behind) if forward else (behind, ahead)
        for slot in range(1, reach + 1):
            if slot <= half:
                source, peer = slot - 1, onward[0]
            elif slot == reach:
                source, peer = 0, onward[reach - 1]
            else:
                source, peer = slot + 1, backward[0]
            hops[which, slot] = remote(
                ref.at[pl.ds(source * rows, rows)],
                ref.at[pl.ds(slot * rows, rows)],
                ring_send.at[which, slot - 1],
                ring_recv.at[which, slot - 1],
                peer,
            )

    def launch(which):
        hops[which, reach].start()
        hops[which, 1].start()

    def advance(which, step):
        hops[which, step].wait_recv()
        if step < half:
            hops[which, step + 1].start()
        hops[which, reach + 1 - step].wait_recv()
        if reach + 1 - step > half + 1:
            hops[which, reach - step].start()

    norm_copies = [
        remote(sums.at[head], sums.at[head], norm_send.at[t + 1], norm_recv.at[t + 1], peer)
        for t, peer in enumerate(norm_peers)
    ]
    for copy in norm_copies:
        copy.start()
    launch(values)
    launch(grads)

    for copy in norm_copies:
        copy.wait_recv()
    total = sums[0]
    for h in range(1, head_total):
        total = total + sums[h]
    inverse = lax.rsqrt(total / (head_total * (NEAR + 1) * HD) + EPSILON)
    q_scale = jnp.broadcast_to(inverse[0:1, :], (rows, rows)).T
    k_scale = jnp.broadcast_to(inverse[1:2, :], (rows, rows)).T
    k_normed = [
        rounded(part * k_scale * kgain_ref[:, h * HD : (h + 1) * HD])
        for h, part in enumerate(k_heads)
    ]
    near_k, far_k = split_heads(k_normed, index)
    store_near(ks, near_k, rows)
    q_normed = [
        rounded(part * q_scale * qgain_ref[:, h * HD : (h + 1) * HD])
        for h, part in enumerate(q_heads)
    ]
    near_q, far_q = split_heads(q_normed, index)
    store_near(qs, near_q, rows)
    launch(keys)
    packed = jnp.concatenate(
        [part.reshape(classes, per_peer, HD) for part in (far_q, far_k, far_v, far_g)], axis=1
    )
    far_out[...] = packed.astype(jnp.bfloat16)
    advance(values, 1)
    advance(grads, 1)
    far_copies = [
        remote(far_out.at[far_turns[t]], far_in.at[turn], far_send.at[t + 1], far_recv.at[t + 1], peer)
        for t, peer in enumerate(far_peers)
    ]
    for copy in far_copies:
        copy.start()
    far_in[turn] = far_out[turn]
    advance(keys, 1)
    launch(queries)
    advance(values, 2)
    advance(grads, 2)
    advance(keys, 2)

    for copy in far_copies:
        copy.wait_recv()
    gathered = far_in[...].astype(jnp.float32)
    far_q, far_k, far_v, far_g = [
        gathered[:, a * per_peer : (a + 1) * per_peer, :].reshape(rows, HD).astype(jnp.bfloat16)
        for a in range(4)
    ]
    j = lax.broadcasted_iota(jnp.int32, (rows, rows), 0)
    i = lax.broadcasted_iota(jnp.int32, (rows, rows), 1)
    far_allowed = (j <= i) & (((i - j) & (per_peer - 1)) == 0)
    dq, score_low, weights_low, _, _ = attend(far_q, far_k, far_v, far_g, far_allowed)
    parts = [dq, dot_nn(score_low, far_q) * SCORE_SCALE, dot_nn(weights_low, far_g), jnp.zeros_like(dq)]
    far_res[...] = jnp.concatenate(
        [part.reshape(classes, per_peer, HD) for part in parts], axis=1
    ).astype(jnp.bfloat16)

    advance(values, 3)
    advance(grads, 3)
    advance(keys, 3)
    advance(queries, 1)
    back_copies = [
        remote(far_res.at[far_turns[t]], far_back.at[turn], back_send.at[t + 1], back_recv.at[t + 1], peer)
        for t, peer in enumerate(far_peers)
    ]
    for copy in back_copies:
        copy.start()
    far_back[turn] = far_res[turn]
    advance(values, 4)
    advance(keys, 4)

    span = (reach + 1) * rows

    def query_side(h):
        r = lax.broadcasted_iota(jnp.int32, (span, rows), 0)
        c = lax.broadcasted_iota(jnp.int32, (span, rows), 1)
        block = lax.shift_right_logical(r, int(math.log2(rows)))
        gap = c + block * (2 * rows) - r
        allowed = (gap >= 0) & (gap < WINDOW) & (block <= ctx)
        cut = slice(h * HD, (h + 1) * HD)
        dq, _, _, log_total, delta = attend(
            qs[0:rows, cut], ks[:, cut], vs[:, cut], gs[0:rows, cut], allowed
        )
        dq_near[:, cut] = dq
        stats[0, h : h + 1, :] = log_total
        stats[0, NEAR + h : NEAR + h + 1, :] = delta

    def key_side(o):
        gap = i - j + o * rows
        allowed = (gap >= 0) & (gap < WINDOW) & (i * 0 + (ctx + o) < ctx_count)
        for h in range(NEAR):
            cut = slice(h * HD, (h + 1) * HD)
            q = qs[o * rows : (o + 1) * rows, cut]
            g = gs[o * rows : (o + 1) * rows, cut]
            scores = dot_nt(ks[0:rows, cut], q) * SCORE_SCALE
            weights = jnp.where(allowed, jnp.exp(scores - stats[o, h : h + 1, :]), 0.0)
            score_grads = weights * (
                dot_nt(vs[0:rows, cut], g) - stats[o, NEAR + h : NEAR + h + 1, :]
            )
            dv = dot_nn(weights.astype(jnp.bfloat16), g)
            dk = dot_nn(score_grads.astype(jnp.bfloat16), q)
            if o == 0:
                dv_near[:, cut] = dv
                dk_near[:, cut] = dk
            else:
                dv_near[:, cut] += dv
                dk_near[:, cut] += dk

    query_side(0)
    advance(queries, 2)
    query_side(1)
    advance(queries, 3)
    query_side(2)
    advance(grads, 4)
    stat_copies = {
        o: remote(stats.at[0], stats.at[o], stat_send.at[o], stat_recv.at[o], behind[o - 1])
        for o in range(1, reach + 1)
    }
    for copy in stat_copies.values():
        copy.start()
    key_side(0)

    for copy in back_copies:
        copy.wait_recv()
    back = far_back[...].astype(jnp.float32)
    far = [back[:, a * per_peer : (a + 1) * per_peer, :].reshape(rows, HD) for a in range(3)]

    def put(out, near_ref, remote_part, scale):
        near = [near_ref[:, h * HD : (h + 1) * HD] * scale for h in range(NEAR)]
        for h, part in enumerate(join_heads(near, remote_part, index)):
            out[:, h * HD : (h + 1) * HD] = part.astype(jnp.bfloat16)

    put(q_out, dq_near, far[0], 1.0)
    order = []
    for step in range(1, half):
        order += [step, reach + 1 - step]
    for o in order:
        stat_copies[o].wait_recv()
        key_side(o)
    advance(queries, 4)
    for o in (half, half + 1):
        stat_copies[o].wait_recv()
        key_side(o)
    put(k_out, dk_near, far[1], SCORE_SCALE)
    put(v_out, dv_near, far[2], 1.0)
    sent = norm_copies + far_copies + back_copies + list(stat_copies.values()) + list(hops.values())
    for copy in sent:
        copy.wait_send()


def on_device(
    ctx_count, head_total, raw_queries, raw_keys, values, output_gradient, query_gain, key_gain, head_kind
):
    rows, width = raw_queries.shape
    reach = WINDOW // rows
    classes = ctx_count // (STRIDE // rows)
    quad = 4 * (rows // classes)
    near_width = NEAR * HD
    low, wide = jnp.bfloat16, jnp.float32
    vmem = pl.BlockSpec(memory_space=pltpu.VMEM)
    smem = pl.BlockSpec(memory_space=pltpu.SMEM)
    dma = pltpu.SemaphoreType.DMA
    result = jax.ShapeDtypeStruct((rows, width), low)
    return pl.pallas_call(
        functools.partial(backward_kernel, ctx_count, head_total),
        name="backward",
        out_shape=(result,) * 3,
        in_specs=[smem] + [vmem] * 6,
        out_specs=(vmem,) * 3,
        scratch_shapes=[pltpu.VMEM(((reach + 1) * rows, near_width), low)] * 4
        + [
            pltpu.VMEM((head_total, 8, HD), wide),
            pltpu.VMEM((reach + 1, 8, HD), wide),
        ]
        + [pltpu.VMEM((classes, quad, HD), low)] * 4
        + [pltpu.VMEM((rows, near_width), wide)] * 3
        + [dma((4, reach))] * 2
        + [dma((head_total,))] * 2
        + [dma((classes,))] * 4
        + [dma((reach + 1,))] * 2,
        compiler_params=pltpu.CompilerParams(collective_id=0, has_side_effects=True),
    )(
        head_kind, raw_queries, raw_keys, values, output_gradient,
        query_gain.reshape(1, width), key_gain.reshape(1, width),
    )


def solution(mesh):
    both = P("ctx", "head")
    placed = (both, both, both, both, P("head"), P("head"), P("head"))
    return jax.shard_map(
        functools.partial(on_device, mesh.shape["ctx"], mesh.shape["head"]),
        mesh=mesh,
        in_specs=placed,
        out_specs=(both, both, both),
        check_vma=False,
    )
```

```python
import functools
import math

import jax
import jax.numpy as jnp
from jax import lax
from jax.experimental import pallas as pl
from jax.experimental.pallas import tpu as pltpu
from jax.sharding import PartitionSpec as P

HD = 128
WINDOW = 1024
STRIDE = 1024
EPSILON = 1e-06
NEAR = 3
MESH = pl.DeviceIdType.MESH
SCORE_SCALE = 1.0 / math.sqrt(HD)


def dot_nt(a, b):
    return lax.dot_general(a, b, (((1,), (1,)), ((), ())), preferred_element_type=jnp.float32)


def dot_tn(a, b):
    return lax.dot_general(a, b, (((0,), (0,)), ((), ())), preferred_element_type=jnp.float32)


def dot_nn(a, b):
    return lax.dot_general(a, b, (((1,), (0,)), ((), ())), preferred_element_type=jnp.float32)


def strided_index(kind_ref):
    index = kind_ref[1] + 2 * kind_ref[2] + 3 * kind_ref[3]
    return jnp.full((1, HD), index, jnp.int32)


def split_heads(heads, index):
    near = [jnp.where(index > g, heads[g], heads[g + 1]) for g in range(NEAR)]
    far = heads[NEAR]
    for g in range(NEAR):
        far = jnp.where(index == g, heads[g], far)
    return near, far


def join_heads(near, far, index):
    joined = []
    for h in range(NEAR + 1):
        if h == 0:
            kept = near[0]
            joined.append(jnp.where(index == 0, far, kept))
        elif h == NEAR:
            joined.append(jnp.where(index == h, far, near[h - 1]))
        else:
            joined.append(
                jnp.where(index == h, far, jnp.where(index > h, near[h], near[h - 1]))
            )
    return joined


def heads_of(ref):
    return [ref[:, h * HD : (h + 1) * HD].astype(jnp.float32) for h in range(NEAR + 1)]


def rounded(array):
    return array.astype(jnp.bfloat16).astype(jnp.float32)


def square_row(heads):
    total = heads[0] * heads[0]
    for part in heads[1:]:
        total = total + part * part
    column = jnp.sum(total, axis=1, keepdims=True)
    return jnp.broadcast_to(column, total.shape).T[0:1, :]


def store_near(ref, near, rows):
    for g in range(NEAR):
        ref[0:rows, g * HD : (g + 1) * HD] = near[g].astype(jnp.bfloat16)


def place(coordinate, ctx_count):
    return {"ctx": lax.rem(coordinate + ctx_count, ctx_count)}


def attend(q, k, v, g, allowed):
    scores = jnp.where(allowed, dot_nt(k, q) * SCORE_SCALE, -jnp.inf)
    top = jnp.max(scores, axis=0, keepdims=True)
    grown = jnp.exp(scores - top)
    total = jnp.sum(grown, axis=0, keepdims=True)
    weights = grown * (1.0 / total)
    weights_low = weights.astype(jnp.bfloat16)
    weight_grads = dot_nt(v, g)
    delta = jnp.sum(weights_low.astype(jnp.float32) * weight_grads, axis=0, keepdims=True)
    score_low = (weights * (weight_grads - delta)).astype(jnp.bfloat16)
    dq = dot_tn(score_low, k) * SCORE_SCALE
    return dq, score_low, weights_low, top + jnp.log(total), delta


def backward_kernel(
    ctx_count, head_total, kind_ref, q_ref, k_ref, v_ref, g_ref, qgain_ref, kgain_ref,
    q_out, k_out, v_out,
    qs, ks, vs, gs, sums, stats, far_out, far_in, far_res, far_back, dq_near, dk_near, dv_near,
    ring_send, ring_recv, norm_send, norm_recv, far_send, far_recv, back_send, back_recv,
    stat_send, stat_recv, bounce, bounce_send, bounce_recv,
):
    rows = q_ref.shape[0]
    reach = WINDOW // rows
    half = reach // 2
    period = STRIDE // rows
    classes = ctx_count // period
    per_peer = rows // classes
    ctx = lax.axis_index("ctx")
    head = lax.axis_index("head")
    column = lax.rem(ctx, period)
    turn = lax.div(ctx, period)
    norm_peers = [{"head": lax.rem(head + t, head_total)} for t in range(1, head_total)]
    far_turns = [lax.rem(turn + t, classes) for t in range(1, classes)]
    far_peers = [{"ctx": t * period + column} for t in far_turns]
    ahead = [place(ctx + o, ctx_count) for o in range(1, reach + 1)]
    behind = [place(ctx - o, ctx_count) for o in range(1, reach + 1)]

    barrier = pltpu.get_barrier_semaphore()
    greeted = ahead + behind + norm_peers + far_peers
    for peer in greeted:
        pl.semaphore_signal(barrier, inc=1, device_id=peer, device_id_type=MESH)

    index = strided_index(kind_ref)
    near_v, far_v = split_heads(heads_of(v_ref), index)
    near_g, far_g = split_heads(heads_of(g_ref), index)
    store_near(vs, near_v, rows)
    store_near(gs, near_g, rows)
    q_heads = heads_of(q_ref)
    k_heads = heads_of(k_ref)
    sums[head] = jnp.concatenate(
        [square_row(q_heads), square_row(k_heads), jnp.zeros((6, HD), jnp.float32)], axis=0
    )
    stats[0] = jnp.zeros((8, HD), jnp.float32)
    pl.semaphore_wait(barrier, len(greeted))

    def remote(src, dst, send_sem, recv_sem, peer):
        return pltpu.make_async_remote_copy(
            src_ref=src, dst_ref=dst, send_sem=send_sem, recv_sem=recv_sem,
            device_id=peer, device_id_type=MESH,
        )

    values, grads, keys, queries = range(4)
    first_column = column == 0
    last_column = column == period - 1
    hops, edges, passes = {}, {}, {}
    for which, ref, forward, y_first in (
        (values, vs, True, True),
        (grads, gs, False, False),
        (keys, ks, True, False),
        (queries, qs, False, True),
    ):
        onward, backward = (ahead, behind) if forward else (behind, ahead)
        for slot in range(1, reach + 1):
            source = slot - 1 if slot <= half else (0 if slot == reach else slot + 1)
            piece = ref.at[pl.ds(source * rows, rows)]
            landing = ref.at[pl.ds(slot * rows, rows)]
            send, recv = ring_send.at[which, slot - 1], ring_recv.at[which, slot - 1]
            if slot == reach:
                hops[which, slot] = remote(piece, landing, send, recv, onward[reach - 1])
                continue
            here, there = (onward, backward) if slot <= half else (backward, onward)
            hops[which, slot] = remote(piece, landing, send, recv, here[0])
            upward = here is ahead
            near_edge, far_edge = (
                (last_column, first_column) if upward else (first_column, last_column)
            )
            by_row, by_column = here[period - 1], there[period - 2]
            stop = bounce.at[which, slot - 1]
            edges[which, slot] = (
                near_edge,
                remote(
                    piece, stop, send, bounce_recv.at[which, slot - 1],
                    by_row if y_first else by_column,
                ),
            )
            passes[which, slot] = (
                near_edge if y_first else far_edge,
                remote(
                    stop, landing, bounce_send.at[which, slot - 1], recv,
                    by_column if y_first else by_row,
                ),
            )

    def send_on(which, slot):
        at_edge, copy = edges[which, slot]

        @pl.when(at_edge)
        def _():
            copy.start()

        @pl.when(jnp.logical_not(at_edge))
        def _():
            hops[which, slot].start()

    def arrive(which, slot):
        if slot < reach:
            relays, copy = passes[which, slot]

            @pl.when(relays)
            def _():
                edges[which, slot][1].wait_recv()
                copy.start()

        hops[which, slot].wait_recv()

    def launch(which):
        hops[which, reach].start()
        send_on(which, 1)

    def advance(which, step):
        arrive(which, step)
        if step < half:
            send_on(which, step + 1)
        arrive(which, reach + 1 - step)
        if reach + 1 - step > half + 1:
            send_on(which, reach - step)

    norm_copies = [
        remote(sums.at[head], sums.at[head], norm_send.at[t + 1], norm_recv.at[t + 1], peer)
        for t, peer in enumerate(norm_peers)
    ]
    for copy in norm_copies:
        copy.start()
    launch(values)
    launch(grads)

    for copy in norm_copies:
        copy.wait_recv()
    total = sums[0]
    for h in range(1, head_total):
        total = total + sums[h]
    inverse = lax.rsqrt(total / (head_total * (NEAR + 1) * HD) + EPSILON)
    q_scale = jnp.broadcast_to(inverse[0:1, :], (rows, rows)).T
    k_scale = jnp.broadcast_to(inverse[1:2, :], (rows, rows)).T
    k_normed = [
        rounded(part * k_scale * kgain_ref[:, h * HD : (h + 1) * HD])
        for h, part in enumerate(k_heads)
    ]
    near_k, far_k = split_heads(k_normed, index)
    store_near(ks, near_k, rows)
    q_normed = [
        rounded(part * q_scale * qgain_ref[:, h * HD : (h + 1) * HD])
        for h, part in enumerate(q_heads)
    ]
    near_q, far_q = split_heads(q_normed, index)
    store_near(qs, near_q, rows)
    launch(keys)
    packed = jnp.concatenate(
        [part.reshape(classes, per_peer, HD) for part in (far_q, far_k, far_v, far_g)], axis=1
    )
    far_out[...] = packed.astype(jnp.bfloat16)
    advance(values, 1)
    advance(grads, 1)
    far_copies = [
        remote(far_out.at[far_turns[t]], far_in.at[turn], far_send.at[t + 1], far_recv.at[t + 1], peer)
        for t, peer in enumerate(far_peers)
    ]
    for copy in far_copies:
        copy.start()
    far_in[turn] = far_out[turn]
    advance(keys, 1)
    launch(queries)
    advance(values, 2)
    advance(grads, 2)
    advance(keys, 2)

    for copy in far_copies:
        copy.wait_recv()
    gathered = far_in[...].astype(jnp.float32)
    far_q, far_k, far_v, far_g = [
        gathered[:, a * per_peer : (a + 1) * per_peer, :].reshape(rows, HD).astype(jnp.bfloat16)
        for a in range(4)
    ]
    j = lax.broadcasted_iota(jnp.int32, (rows, rows), 0)
    i = lax.broadcasted_iota(jnp.int32, (rows, rows), 1)
    far_allowed = (j <= i) & (((i - j) & (per_peer - 1)) == 0)
    dq, score_low, weights_low, _, _ = attend(far_q, far_k, far_v, far_g, far_allowed)
    parts = [dq, dot_nn(score_low, far_q) * SCORE_SCALE, dot_nn(weights_low, far_g), jnp.zeros_like(dq)]
    far_res[...] = jnp.concatenate(
        [part.reshape(classes, per_peer, HD) for part in parts], axis=1
    ).astype(jnp.bfloat16)

    advance(values, 3)
    advance(grads, 3)
    advance(keys, 3)
    advance(queries, 1)
    back_copies = [
        remote(far_res.at[far_turns[t]], far_back.at[turn], back_send.at[t + 1], back_recv.at[t + 1], peer)
        for t, peer in enumerate(far_peers)
    ]
    for copy in back_copies:
        copy.start()
    far_back[turn] = far_res[turn]
    advance(values, 4)
    advance(keys, 4)

    span = (reach + 1) * rows

    def query_side(h):
        r = lax.broadcasted_iota(jnp.int32, (span, rows), 0)
        c = lax.broadcasted_iota(jnp.int32, (span, rows), 1)
        block = lax.shift_right_logical(r, int(math.log2(rows)))
        gap = c + block * (2 * rows) - r
        allowed = (gap >= 0) & (gap < WINDOW) & (block <= ctx)
        cut = slice(h * HD, (h + 1) * HD)
        dq, _, _, log_total, delta = attend(
            qs[0:rows, cut], ks[:, cut], vs[:, cut], gs[0:rows, cut], allowed
        )
        dq_near[:, cut] = dq
        stats[0, h : h + 1, :] = log_total
        stats[0, NEAR + h : NEAR + h + 1, :] = delta

    def key_side(o):
        gap = i - j + o * rows
        allowed = (gap >= 0) & (gap < WINDOW) & (i * 0 + (ctx + o) < ctx_count)
        for h in range(NEAR):
            cut = slice(h * HD, (h + 1) * HD)
            q = qs[o * rows : (o + 1) * rows, cut]
            g = gs[o * rows : (o + 1) * rows, cut]
            scores = dot_nt(ks[0:rows, cut], q) * SCORE_SCALE
            weights = jnp.where(allowed, jnp.exp(scores - stats[o, h : h + 1, :]), 0.0)
            score_grads = weights * (
                dot_nt(vs[0:rows, cut], g) - stats[o, NEAR + h : NEAR + h + 1, :]
            )
            dv = dot_nn(weights.astype(jnp.bfloat16), g)
            dk = dot_nn(score_grads.astype(jnp.bfloat16), q)
            if o == 0:
                dv_near[:, cut] = dv
                dk_near[:, cut] = dk
            else:
                dv_near[:, cut] += dv
                dk_near[:, cut] += dk

    query_side(0)
    advance(queries, 2)
    query_side(1)
    advance(queries, 3)
    query_side(2)
    advance(grads, 4)
    stat_copies = {
        o: remote(stats.at[0], stats.at[o], stat_send.at[o], stat_recv.at[o], behind[o - 1])
        for o in range(1, reach + 1)
    }
    for copy in stat_copies.values():
        copy.start()
    key_side(0)

    for copy in back_copies:
        copy.wait_recv()
    back = far_back[...].astype(jnp.float32)
    far = [back[:, a * per_peer : (a + 1) * per_peer, :].reshape(rows, HD) for a in range(3)]

    def put(out, near_ref, remote_part, scale):
        near = [near_ref[:, h * HD : (h + 1) * HD] * scale for h in range(NEAR)]
        for h, part in enumerate(join_heads(near, remote_part, index)):
            out[:, h * HD : (h + 1) * HD] = part.astype(jnp.bfloat16)

    put(q_out, dq_near, far[0], 1.0)
    order = []
    for step in range(1, half):
        order += [step, reach + 1 - step]
    for o in order:
        stat_copies[o].wait_recv()
        key_side(o)
    advance(queries, 4)
    for o in (half, half + 1):
        stat_copies[o].wait_recv()
        key_side(o)
    put(k_out, dk_near, far[1], SCORE_SCALE)
    put(v_out, dv_near, far[2], 1.0)
    sent = norm_copies + far_copies + back_copies + list(stat_copies.values()) + list(hops.values())
    for copy in sent:
        copy.wait_send()
    for relays, copy in passes.values():
        pl.when(relays)(copy.wait_send)


def on_device(
    ctx_count, head_total, raw_queries, raw_keys, values, output_gradient, query_gain, key_gain, head_kind
):
    rows, width = raw_queries.shape
    reach = WINDOW // rows
    classes = ctx_count // (STRIDE // rows)
    quad = 4 * (rows // classes)
    near_width = NEAR * HD
    low, wide = jnp.bfloat16, jnp.float32
    vmem = pl.BlockSpec(memory_space=pltpu.VMEM)
    smem = pl.BlockSpec(memory_space=pltpu.SMEM)
    dma = pltpu.SemaphoreType.DMA
    result = jax.ShapeDtypeStruct((rows, width), low)
    return pl.pallas_call(
        functools.partial(backward_kernel, ctx_count, head_total),
        name="backward",
        out_shape=(result,) * 3,
        in_specs=[smem] + [vmem] * 6,
        out_specs=(vmem,) * 3,
        scratch_shapes=[pltpu.VMEM(((reach + 1) * rows, near_width), low)] * 4
        + [
            pltpu.VMEM((head_total, 8, HD), wide),
            pltpu.VMEM((reach + 1, 8, HD), wide),
        ]
        + [pltpu.VMEM((classes, quad, HD), low)] * 4
        + [pltpu.VMEM((rows, near_width), wide)] * 3
        + [dma((4, reach))] * 2
        + [dma((head_total,))] * 2
        + [dma((classes,))] * 4
        + [dma((reach + 1,))] * 2
        + [pltpu.VMEM((4, reach - 1, rows, near_width), low)]
        + [dma((4, reach - 1))] * 2,
        compiler_params=pltpu.CompilerParams(collective_id=0, has_side_effects=True),
    )(
        head_kind, raw_queries, raw_keys, values, output_gradient,
        query_gain.reshape(1, width), key_gain.reshape(1, width),
    )


def solution(mesh):
    both = P("ctx", "head")
    placed = (both, both, both, both, P("head"), P("head"), P("head"))
    return jax.shard_map(
        functools.partial(on_device, mesh.shape["ctx"], mesh.shape["head"]),
        mesh=mesh,
        in_specs=placed,
        out_specs=(both, both, both),
        check_vma=False,
    )
```

```python
import functools
import math

import jax
import jax.numpy as jnp
from jax import lax
from jax.experimental import pallas as pl
from jax.experimental.pallas import tpu as pltpu
from jax.sharding import PartitionSpec as P

HD = 128
WINDOW = 1024
STRIDE = 1024
EPSILON = 1e-06
NEAR = 3
MESH = pl.DeviceIdType.MESH
SCORE_SCALE = 1.0 / math.sqrt(HD)


def dot_nt(a, b):
    return lax.dot_general(a, b, (((1,), (1,)), ((), ())), preferred_element_type=jnp.float32)


def dot_tn(a, b):
    return lax.dot_general(a, b, (((0,), (0,)), ((), ())), preferred_element_type=jnp.float32)


def dot_nn(a, b):
    return lax.dot_general(a, b, (((1,), (0,)), ((), ())), preferred_element_type=jnp.float32)


def strided_index(kind_ref):
    index = kind_ref[1] + 2 * kind_ref[2] + 3 * kind_ref[3]
    return jnp.full((1, HD), index, jnp.int32)


def split_heads(heads, index):
    near = [jnp.where(index > g, heads[g], heads[g + 1]) for g in range(NEAR)]
    far = heads[NEAR]
    for g in range(NEAR):
        far = jnp.where(index == g, heads[g], far)
    return near, far


def join_heads(near, far, index):
    joined = []
    for h in range(NEAR + 1):
        if h == 0:
            kept = near[0]
            joined.append(jnp.where(index == 0, far, kept))
        elif h == NEAR:
            joined.append(jnp.where(index == h, far, near[h - 1]))
        else:
            joined.append(
                jnp.where(index == h, far, jnp.where(index > h, near[h], near[h - 1]))
            )
    return joined


def heads_of(ref):
    return [ref[:, h * HD : (h + 1) * HD].astype(jnp.float32) for h in range(NEAR + 1)]


def rounded(array):
    return array.astype(jnp.bfloat16).astype(jnp.float32)


def square_row(heads):
    total = heads[0] * heads[0]
    for part in heads[1:]:
        total = total + part * part
    column = jnp.sum(total, axis=1, keepdims=True)
    return jnp.broadcast_to(column, total.shape).T[0:1, :]


def store_near(ref, near, rows):
    for g in range(NEAR):
        ref[0:rows, g * HD : (g + 1) * HD] = near[g].astype(jnp.bfloat16)


def place(coordinate, ctx_count):
    return {"ctx": lax.rem(coordinate + ctx_count, ctx_count)}


def attend(q, k, v, g, allowed):
    return weigh(dot_nt(k, q) * SCORE_SCALE, dot_nt(v, g), k, allowed)


def weigh(scores, weight_grads, k, allowed):
    scores = jnp.where(allowed, scores, -jnp.inf)
    top = jnp.max(scores, axis=0, keepdims=True)
    grown = jnp.exp(scores - top)
    total = jnp.sum(grown, axis=0, keepdims=True)
    weights = grown * (1.0 / total)
    weights_low = weights.astype(jnp.bfloat16)
    delta = jnp.sum(weights_low.astype(jnp.float32) * weight_grads, axis=0, keepdims=True)
    score_low = (weights * (weight_grads - delta)).astype(jnp.bfloat16)
    dq = dot_tn(score_low, k) * SCORE_SCALE
    return dq, score_low, weights_low, top + jnp.log(total), delta


def backward_kernel(
    ctx_count, head_total, kind_ref, q_ref, k_ref, v_ref, g_ref, qgain_ref, kgain_ref,
    q_out, k_out, v_out,
    qs, ks, vs, gs, sums, stats, far_out, far_in, far_res, far_back, dq_near, dk_near, dv_near,
    ring_send, ring_recv, norm_send, norm_recv, far_send, far_recv, back_send, back_recv,
    stat_send, stat_recv, query_scores, query_grads, key_scores, key_grads,
):
    rows = q_ref.shape[0]
    reach = WINDOW // rows
    period = STRIDE // rows
    classes = ctx_count // period
    per_peer = rows // classes
    ctx = lax.axis_index("ctx")
    head = lax.axis_index("head")
    column = lax.rem(ctx, period)
    turn = lax.div(ctx, period)
    norm_peers = [{"head": lax.rem(head + t, head_total)} for t in range(1, head_total)]
    far_turns = [lax.rem(turn + t, classes) for t in range(1, classes)]
    far_peers = [{"ctx": t * period + column} for t in far_turns]
    ahead = [place(ctx + o, ctx_count) for o in range(1, reach + 1)]
    behind = [place(ctx - o, ctx_count) for o in range(1, reach + 1)]

    barrier = pltpu.get_barrier_semaphore()
    greeted = ahead + behind + norm_peers + far_peers
    for peer in greeted:
        pl.semaphore_signal(barrier, inc=1, device_id=peer, device_id_type=MESH)

    index = strided_index(kind_ref)
    near_v, far_v = split_heads(heads_of(v_ref), index)
    near_g, far_g = split_heads(heads_of(g_ref), index)
    store_near(vs, near_v, rows)
    store_near(gs, near_g, rows)
    q_heads = heads_of(q_ref)
    k_heads = heads_of(k_ref)
    sums[head] = jnp.concatenate(
        [square_row(q_heads), square_row(k_heads), jnp.zeros((6, HD), jnp.float32)], axis=0
    )
    stats[0] = jnp.zeros((8, HD), jnp.float32)
    pl.semaphore_wait(barrier, len(greeted))

    def remote(src, dst, send_sem, recv_sem, peer):
        return pltpu.make_async_remote_copy(
            src_ref=src, dst_ref=dst, send_sem=send_sem, recv_sem=recv_sem,
            device_id=peer, device_id_type=MESH,
        )

    values, grads, keys, queries = range(4)
    hops = {}
    for which, ref, forward in (
        (values, vs, True), (grads, gs, False), (keys, ks, True), (queries, qs, False)
    ):
        peer = ahead[0] if forward else behind[0]
        for slot in range(1, reach + 1):
            source = slot - 1
            hops[which, slot] = remote(
                ref.at[pl.ds(source * rows, rows)],
                ref.at[pl.ds(slot * rows, rows)],
                ring_send.at[which, slot - 1],
                ring_recv.at[which, slot - 1],
                peer,
            )

    def advance(which, step):
        hops[which, step].wait_recv()
        if step < reach:
            hops[which, step + 1].start()

    norm_copies = [
        remote(sums.at[head], sums.at[head], norm_send.at[t + 1], norm_recv.at[t + 1], peer)
        for t, peer in enumerate(norm_peers)
    ]
    for copy in norm_copies:
        copy.start()
    hops[values, 1].start()
    hops[grads, 1].start()

    for copy in norm_copies:
        copy.wait_recv()
    total = sums[0]
    for h in range(1, head_total):
        total = total + sums[h]
    inverse = lax.rsqrt(total / (head_total * (NEAR + 1) * HD) + EPSILON)
    q_scale = jnp.broadcast_to(inverse[0:1, :], (rows, rows)).T
    k_scale = jnp.broadcast_to(inverse[1:2, :], (rows, rows)).T
    k_normed = [
        rounded(part * k_scale * kgain_ref[:, h * HD : (h + 1) * HD])
        for h, part in enumerate(k_heads)
    ]
    near_k, far_k = split_heads(k_normed, index)
    store_near(ks, near_k, rows)
    q_normed = [
        rounded(part * q_scale * qgain_ref[:, h * HD : (h + 1) * HD])
        for h, part in enumerate(q_heads)
    ]
    near_q, far_q = split_heads(q_normed, index)
    store_near(qs, near_q, rows)
    hops[keys, 1].start()
    hops[queries, 1].start()
    packed = jnp.concatenate(
        [part.reshape(classes, per_peer, HD) for part in (far_q, far_k, far_v, far_g)], axis=1
    )
    far_out[...] = packed.astype(jnp.bfloat16)
    far_copies = [
        remote(far_out.at[far_turns[t]], far_in.at[turn], far_send.at[t + 1], far_recv.at[t + 1], peer)
        for t, peer in enumerate(far_peers)
    ]
    for copy in far_copies:
        copy.start()
    far_in[turn] = far_out[turn]
    j = lax.broadcasted_iota(jnp.int32, (rows, rows), 0)
    i = lax.broadcasted_iota(jnp.int32, (rows, rows), 1)
    span = (reach + 1) * rows

    def products(o):
        block = slice(o * rows, (o + 1) * rows)
        for h in range(NEAR):
            cut = slice(h * HD, (h + 1) * HD)
            own_q, own_k, own_v, own_g = qs[0:rows, cut], ks[0:rows, cut], vs[0:rows, cut], gs[0:rows, cut]
            query_scores[h, block, :] = dot_nt(ks[block, cut], own_q) * SCORE_SCALE
            query_grads[h, block, :] = dot_nt(vs[block, cut], own_g)
            key_scores[h, block, :] = dot_nt(own_k, qs[block, cut]) * SCORE_SCALE
            key_grads[h, block, :] = dot_nt(own_v, gs[block, cut])

    def ring_step(step):
        for which in (values, grads, keys, queries):
            advance(which, step)
        products(step)

    products(0)
    ring_step(1)
    ring_step(2)

    for copy in far_copies:
        copy.wait_recv()
    gathered = far_in[...].astype(jnp.float32)
    far_q, far_k, far_v, far_g = [
        gathered[:, a * per_peer : (a + 1) * per_peer, :].reshape(rows, HD).astype(jnp.bfloat16)
        for a in range(4)
    ]
    far_allowed = (j <= i) & (((i - j) & (per_peer - 1)) == 0)
    dq, score_low, weights_low, _, _ = attend(far_q, far_k, far_v, far_g, far_allowed)
    parts = [dq, dot_nn(score_low, far_q) * SCORE_SCALE, dot_nn(weights_low, far_g), jnp.zeros_like(dq)]
    far_res[...] = jnp.concatenate(
        [part.reshape(classes, per_peer, HD) for part in parts], axis=1
    ).astype(jnp.bfloat16)

    ring_step(3)
    back_copies = [
        remote(far_res.at[far_turns[t]], far_back.at[turn], back_send.at[t + 1], back_recv.at[t + 1], peer)
        for t, peer in enumerate(far_peers)
    ]
    for copy in back_copies:
        copy.start()
    far_back[turn] = far_res[turn]
    for step in range(4, reach + 1):
        ring_step(step)

    def query_side(h):
        r = lax.broadcasted_iota(jnp.int32, (span, rows), 0)
        c = lax.broadcasted_iota(jnp.int32, (span, rows), 1)
        block = lax.shift_right_logical(r, int(math.log2(rows)))
        gap = c + block * (2 * rows) - r
        allowed = (gap >= 0) & (gap < WINDOW) & (block <= ctx)
        cut = slice(h * HD, (h + 1) * HD)
        dq, _, _, log_total, delta = weigh(query_scores[h], query_grads[h], ks[:, cut], allowed)
        dq_near[:, cut] = dq
        stats[0, h : h + 1, :] = log_total
        stats[0, NEAR + h : NEAR + h + 1, :] = delta

    def key_side(o):
        gap = i - j + o * rows
        allowed = (gap >= 0) & (gap < WINDOW) & (i * 0 + (ctx + o) < ctx_count)
        for h in range(NEAR):
            cut = slice(h * HD, (h + 1) * HD)
            q = qs[o * rows : (o + 1) * rows, cut]
            g = gs[o * rows : (o + 1) * rows, cut]
            block = slice(o * rows, (o + 1) * rows)
            weights = jnp.where(allowed, jnp.exp(key_scores[h, block, :] - stats[o, h : h + 1, :]), 0.0)
            score_grads = weights * (
                key_grads[h, block, :] - stats[o, NEAR + h : NEAR + h + 1, :]
            )
            dv = dot_nn(weights.astype(jnp.bfloat16), g)
            dk = dot_nn(score_grads.astype(jnp.bfloat16), q)
            if o == 0:
                dv_near[:, cut] = dv
                dk_near[:, cut] = dk
            else:
                dv_near[:, cut] += dv
                dk_near[:, cut] += dk

    for h in range(NEAR):
        query_side(h)
    for copy in back_copies:
        copy.wait_recv()
    back = far_back[...].astype(jnp.float32)
    far = [back[:, a * per_peer : (a + 1) * per_peer, :].reshape(rows, HD) for a in range(3)]

    def put(out, near_ref, remote_part, scale):
        near = [near_ref[:, h * HD : (h + 1) * HD] * scale for h in range(NEAR)]
        for h, part in enumerate(join_heads(near, remote_part, index)):
            out[:, h * HD : (h + 1) * HD] = part.astype(jnp.bfloat16)

    put(q_out, dq_near, far[0], 1.0)
    stat_copies = {
        o: remote(stats.at[0], stats.at[o], stat_send.at[o], stat_recv.at[o], behind[o - 1])
        for o in range(1, reach + 1)
    }
    for copy in stat_copies.values():
        copy.start()
    key_side(0)

    for o in range(1, reach + 1):
        stat_copies[o].wait_recv()
        key_side(o)
    put(k_out, dk_near, far[1], SCORE_SCALE)
    put(v_out, dv_near, far[2], 1.0)
    sent = norm_copies + far_copies + back_copies + list(stat_copies.values()) + list(hops.values())
    for copy in sent:
        copy.wait_send()


def on_device(
    ctx_count, head_total, raw_queries, raw_keys, values, output_gradient, query_gain, key_gain, head_kind
):
    rows, width = raw_queries.shape
    reach = WINDOW // rows
    classes = ctx_count // (STRIDE // rows)
    quad = 4 * (rows // classes)
    near_width = NEAR * HD
    low, wide = jnp.bfloat16, jnp.float32
    vmem = pl.BlockSpec(memory_space=pltpu.VMEM)
    smem = pl.BlockSpec(memory_space=pltpu.SMEM)
    dma = pltpu.SemaphoreType.DMA
    result = jax.ShapeDtypeStruct((rows, width), low)
    return pl.pallas_call(
        functools.partial(backward_kernel, ctx_count, head_total),
        name="backward",
        out_shape=(result,) * 3,
        in_specs=[smem] + [vmem] * 6,
        out_specs=(vmem,) * 3,
        scratch_shapes=[pltpu.VMEM(((reach + 1) * rows, near_width), low)] * 4
        + [
            pltpu.VMEM((head_total, 8, HD), wide),
            pltpu.VMEM((reach + 1, 8, HD), wide),
        ]
        + [pltpu.VMEM((classes, quad, HD), low)] * 4
        + [pltpu.VMEM((rows, near_width), wide)] * 3
        + [dma((4, reach))] * 2
        + [dma((head_total,))] * 2
        + [dma((classes,))] * 4
        + [dma((reach + 1,))] * 2
        + [pltpu.VMEM((NEAR, (reach + 1) * rows, rows), wide)] * 4,
        compiler_params=pltpu.CompilerParams(collective_id=0, has_side_effects=True),
    )(
        head_kind, raw_queries, raw_keys, values, output_gradient,
        query_gain.reshape(1, width), key_gain.reshape(1, width),
    )


def solution(mesh):
    both = P("ctx", "head")
    placed = (both, both, both, both, P("head"), P("head"), P("head"))
    return jax.shard_map(
        functools.partial(on_device, mesh.shape["ctx"], mesh.shape["head"]),
        mesh=mesh,
        in_specs=placed,
        out_specs=(both, both, both),
        check_vma=False,
    )
```

```python
import functools
import math

import jax
import jax.numpy as jnp
from jax import lax
from jax.experimental import pallas as pl
from jax.experimental.pallas import tpu as pltpu
from jax.sharding import PartitionSpec as P

HD = 128
WINDOW = 1024
STRIDE = 1024
EPSILON = 1e-06
NEAR = 3
PIECES = 2
MESH = pl.DeviceIdType.MESH
SCORE_SCALE = 1.0 / math.sqrt(HD)


def dot_nt(a, b):
    return lax.dot_general(a, b, (((1,), (1,)), ((), ())), preferred_element_type=jnp.float32)


def dot_tn(a, b):
    return lax.dot_general(a, b, (((0,), (0,)), ((), ())), preferred_element_type=jnp.float32)


def dot_nn(a, b):
    return lax.dot_general(a, b, (((1,), (0,)), ((), ())), preferred_element_type=jnp.float32)


def strided_index(kind_ref):
    index = kind_ref[1] + 2 * kind_ref[2] + 3 * kind_ref[3]
    return jnp.full((1, HD), index, jnp.int32)


def split_heads(heads, index):
    near = [jnp.where(index > g, heads[g], heads[g + 1]) for g in range(NEAR)]
    far = heads[NEAR]
    for g in range(NEAR):
        far = jnp.where(index == g, heads[g], far)
    return near, far


def join_heads(near, far, index):
    joined = []
    for h in range(NEAR + 1):
        if h == 0:
            kept = near[0]
            joined.append(jnp.where(index == 0, far, kept))
        elif h == NEAR:
            joined.append(jnp.where(index == h, far, near[h - 1]))
        else:
            joined.append(
                jnp.where(index == h, far, jnp.where(index > h, near[h], near[h - 1]))
            )
    return joined


def heads_of(ref):
    return [ref[:, h * HD : (h + 1) * HD].astype(jnp.float32) for h in range(NEAR + 1)]


def rounded(array):
    return array.astype(jnp.bfloat16).astype(jnp.float32)


def square_row(heads):
    total = heads[0] * heads[0]
    for part in heads[1:]:
        total = total + part * part
    column = jnp.sum(total, axis=1, keepdims=True)
    return jnp.broadcast_to(column, total.shape).T[0:1, :]


def store_near(ref, near, rows):
    for g in range(NEAR):
        ref[0:rows, g * HD : (g + 1) * HD] = near[g].astype(jnp.bfloat16)


def place(coordinate, ctx_count):
    return {"ctx": lax.rem(coordinate + ctx_count, ctx_count)}


def attend(q, k, v, g, allowed):
    return weigh(dot_nt(k, q) * SCORE_SCALE, dot_nt(v, g), k, allowed)


def weigh(scores, weight_grads, k, allowed):
    scores = jnp.where(allowed, scores, -jnp.inf)
    top = jnp.max(scores, axis=0, keepdims=True)
    grown = jnp.exp(scores - top)
    total = jnp.sum(grown, axis=0, keepdims=True)
    weights = grown * (1.0 / total)
    weights_low = weights.astype(jnp.bfloat16)
    delta = jnp.sum(weights_low.astype(jnp.float32) * weight_grads, axis=0, keepdims=True)
    score_low = (weights * (weight_grads - delta)).astype(jnp.bfloat16)
    dq = dot_tn(score_low, k) * SCORE_SCALE
    return dq, score_low, weights_low, top + jnp.log(total), delta


def backward_kernel(
    ctx_count, head_total, kind_ref, q_ref, k_ref, v_ref, g_ref, qgain_ref, kgain_ref,
    q_out, k_out, v_out,
    qs, ks, vs, gs, sums, stats, far_out, far_in, far_res, far_back, dq_near, dk_near, dv_near,
    ring_send, ring_recv, norm_send, norm_recv, far_send, far_recv, back_send, back_recv,
    stat_send, stat_recv, query_scores, query_grads, key_scores, key_grads,
):
    rows = q_ref.shape[0]
    reach = WINDOW // rows
    period = STRIDE // rows
    classes = ctx_count // period
    per_peer = rows // classes
    ctx = lax.axis_index("ctx")
    head = lax.axis_index("head")
    column = lax.rem(ctx, period)
    turn = lax.div(ctx, period)
    norm_peers = [{"head": lax.rem(head + t, head_total)} for t in range(1, head_total)]
    far_turns = [lax.rem(turn + t, classes) for t in range(1, classes)]
    far_peers = [{"ctx": t * period + column} for t in far_turns]
    ahead = [place(ctx + o, ctx_count) for o in range(1, reach + 1)]
    behind = [place(ctx - o, ctx_count) for o in range(1, reach + 1)]

    barrier = pltpu.get_barrier_semaphore()
    greeted = ahead + behind + norm_peers + far_peers
    for peer in greeted:
        pl.semaphore_signal(barrier, inc=1, device_id=peer, device_id_type=MESH)

    index = strided_index(kind_ref)
    near_v, far_v = split_heads(heads_of(v_ref), index)
    near_g, far_g = split_heads(heads_of(g_ref), index)
    store_near(vs, near_v, rows)
    store_near(gs, near_g, rows)
    q_heads = heads_of(q_ref)
    k_heads = heads_of(k_ref)
    sums[head] = jnp.concatenate(
        [square_row(q_heads), square_row(k_heads), jnp.zeros((6, HD), jnp.float32)], axis=0
    )
    stats[0] = jnp.zeros((8, HD), jnp.float32)
    pl.semaphore_wait(barrier, len(greeted))

    def remote(src, dst, send_sem, recv_sem, peer):
        return pltpu.make_async_remote_copy(
            src_ref=src, dst_ref=dst, send_sem=send_sem, recv_sem=recv_sem,
            device_id=peer, device_id_type=MESH,
        )

    values, grads, keys, queries = range(4)
    hops = {}
    size = rows // PIECES
    for which, ref, forward in (
        (values, vs, True), (grads, gs, False), (keys, ks, True), (queries, qs, False)
    ):
        peer = ahead[0] if forward else behind[0]
        for slot in range(1, reach + 1):
            for piece in range(PIECES):
                start = slot * rows + piece * size
                number = (slot - 1) * PIECES + piece
                hops[which, slot, piece] = remote(
                    ref.at[pl.ds(start - rows, size)],
                    ref.at[pl.ds(start, size)],
                    ring_send.at[which, number],
                    ring_recv.at[which, number],
                    peer,
                )

    def launch(*chosen):
        for piece in range(PIECES):
            for which in chosen:
                hops[which, 1, piece].start()

    def advance(step, *chosen):
        for piece in range(PIECES):
            for which in chosen:
                hops[which, step, piece].wait_recv()
                if step < reach:
                    hops[which, step + 1, piece].start()

    norm_copies = [
        remote(sums.at[head], sums.at[head], norm_send.at[t + 1], norm_recv.at[t + 1], peer)
        for t, peer in enumerate(norm_peers)
    ]
    for copy in norm_copies:
        copy.start()
    launch(values, grads)

    for copy in norm_copies:
        copy.wait_recv()
    total = sums[0]
    for h in range(1, head_total):
        total = total + sums[h]
    inverse = lax.rsqrt(total / (head_total * (NEAR + 1) * HD) + EPSILON)
    q_scale = jnp.broadcast_to(inverse[0:1, :], (rows, rows)).T
    k_scale = jnp.broadcast_to(inverse[1:2, :], (rows, rows)).T
    k_normed = [
        rounded(part * k_scale * kgain_ref[:, h * HD : (h + 1) * HD])
        for h, part in enumerate(k_heads)
    ]
    near_k, far_k = split_heads(k_normed, index)
    store_near(ks, near_k, rows)
    q_normed = [
        rounded(part * q_scale * qgain_ref[:, h * HD : (h + 1) * HD])
        for h, part in enumerate(q_heads)
    ]
    near_q, far_q = split_heads(q_normed, index)
    store_near(qs, near_q, rows)
    launch(keys, queries)
    packed = jnp.concatenate(
        [part.reshape(classes, per_peer, HD) for part in (far_q, far_k, far_v, far_g)], axis=1
    )
    far_out[...] = packed.astype(jnp.bfloat16)
    far_copies = [
        remote(far_out.at[far_turns[t]], far_in.at[turn], far_send.at[t + 1], far_recv.at[t + 1], peer)
        for t, peer in enumerate(far_peers)
    ]
    for copy in far_copies:
        copy.start()
    far_in[turn] = far_out[turn]
    j = lax.broadcasted_iota(jnp.int32, (rows, rows), 0)
    i = lax.broadcasted_iota(jnp.int32, (rows, rows), 1)
    span = (reach + 1) * rows

    def products(o):
        block = slice(o * rows, (o + 1) * rows)
        for h in range(NEAR):
            cut = slice(h * HD, (h + 1) * HD)
            own_q, own_k, own_v, own_g = qs[0:rows, cut], ks[0:rows, cut], vs[0:rows, cut], gs[0:rows, cut]
            query_scores[h, block, :] = dot_nt(ks[block, cut], own_q) * SCORE_SCALE
            query_grads[h, block, :] = dot_nt(vs[block, cut], own_g)
            key_scores[h, block, :] = dot_nt(own_k, qs[block, cut]) * SCORE_SCALE
            key_grads[h, block, :] = dot_nt(own_v, gs[block, cut])

    def ring_step(step):
        advance(step, values, grads)
        advance(step, keys, queries)
        products(step)

    products(0)
    ring_step(1)
    ring_step(2)

    for copy in far_copies:
        copy.wait_recv()
    gathered = far_in[...].astype(jnp.float32)
    far_q, far_k, far_v, far_g = [
        gathered[:, a * per_peer : (a + 1) * per_peer, :].reshape(rows, HD).astype(jnp.bfloat16)
        for a in range(4)
    ]
    far_allowed = (j <= i) & (((i - j) & (per_peer - 1)) == 0)
    dq, score_low, weights_low, _, _ = attend(far_q, far_k, far_v, far_g, far_allowed)
    parts = [dq, dot_nn(score_low, far_q) * SCORE_SCALE, dot_nn(weights_low, far_g), jnp.zeros_like(dq)]
    far_res[...] = jnp.concatenate(
        [part.reshape(classes, per_peer, HD) for part in parts], axis=1
    ).astype(jnp.bfloat16)

    ring_step(3)
    back_copies = [
        remote(far_res.at[far_turns[t]], far_back.at[turn], back_send.at[t + 1], back_recv.at[t + 1], peer)
        for t, peer in enumerate(far_peers)
    ]
    for copy in back_copies:
        copy.start()
    far_back[turn] = far_res[turn]
    for step in range(4, reach + 1):
        ring_step(step)

    def query_side(h):
        r = lax.broadcasted_iota(jnp.int32, (span, rows), 0)
        c = lax.broadcasted_iota(jnp.int32, (span, rows), 1)
        block = lax.shift_right_logical(r, int(math.log2(rows)))
        gap = c + block * (2 * rows) - r
        allowed = (gap >= 0) & (gap < WINDOW) & (block <= ctx)
        cut = slice(h * HD, (h + 1) * HD)
        dq, _, _, log_total, delta = weigh(query_scores[h], query_grads[h], ks[:, cut], allowed)
        dq_near[:, cut] = dq
        stats[0, h : h + 1, :] = log_total
        stats[0, NEAR + h : NEAR + h + 1, :] = delta

    def key_side(o):
        gap = i - j + o * rows
        allowed = (gap >= 0) & (gap < WINDOW) & (i * 0 + (ctx + o) < ctx_count)
        for h in range(NEAR):
            cut = slice(h * HD, (h + 1) * HD)
            q = qs[o * rows : (o + 1) * rows, cut]
            g = gs[o * rows : (o + 1) * rows, cut]
            block = slice(o * rows, (o + 1) * rows)
            weights = jnp.where(allowed, jnp.exp(key_scores[h, block, :] - stats[o, h : h + 1, :]), 0.0)
            score_grads = weights * (
                key_grads[h, block, :] - stats[o, NEAR + h : NEAR + h + 1, :]
            )
            dv = dot_nn(weights.astype(jnp.bfloat16), g)
            dk = dot_nn(score_grads.astype(jnp.bfloat16), q)
            if o == 0:
                dv_near[:, cut] = dv
                dk_near[:, cut] = dk
            else:
                dv_near[:, cut] += dv
                dk_near[:, cut] += dk

    for h in range(NEAR):
        query_side(h)
    for copy in back_copies:
        copy.wait_recv()
    back = far_back[...].astype(jnp.float32)
    far = [back[:, a * per_peer : (a + 1) * per_peer, :].reshape(rows, HD) for a in range(3)]

    def put(out, near_ref, remote_part, scale):
        near = [near_ref[:, h * HD : (h + 1) * HD] * scale for h in range(NEAR)]
        for h, part in enumerate(join_heads(near, remote_part, index)):
            out[:, h * HD : (h + 1) * HD] = part.astype(jnp.bfloat16)

    put(q_out, dq_near, far[0], 1.0)
    stat_copies = {
        o: remote(stats.at[0], stats.at[o], stat_send.at[o], stat_recv.at[o], behind[o - 1])
        for o in range(1, reach + 1)
    }
    for copy in stat_copies.values():
        copy.start()
    key_side(0)

    for o in range(1, reach + 1):
        stat_copies[o].wait_recv()
        key_side(o)
    put(k_out, dk_near, far[1], SCORE_SCALE)
    put(v_out, dv_near, far[2], 1.0)
    sent = norm_copies + far_copies + back_copies + list(stat_copies.values()) + list(hops.values())
    for copy in sent:
        copy.wait_send()


def on_device(
    ctx_count, head_total, raw_queries, raw_keys, values, output_gradient, query_gain, key_gain, head_kind
):
    rows, width = raw_queries.shape
    reach = WINDOW // rows
    classes = ctx_count // (STRIDE // rows)
    quad = 4 * (rows // classes)
    near_width = NEAR * HD
    low, wide = jnp.bfloat16, jnp.float32
    vmem = pl.BlockSpec(memory_space=pltpu.VMEM)
    smem = pl.BlockSpec(memory_space=pltpu.SMEM)
    dma = pltpu.SemaphoreType.DMA
    result = jax.ShapeDtypeStruct((rows, width), low)
    return pl.pallas_call(
        functools.partial(backward_kernel, ctx_count, head_total),
        name="backward",
        out_shape=(result,) * 3,
        in_specs=[smem] + [vmem] * 6,
        out_specs=(vmem,) * 3,
        scratch_shapes=[pltpu.VMEM(((reach + 1) * rows, near_width), low)] * 4
        + [
            pltpu.VMEM((head_total, 8, HD), wide),
            pltpu.VMEM((reach + 1, 8, HD), wide),
        ]
        + [pltpu.VMEM((classes, quad, HD), low)] * 4
        + [pltpu.VMEM((rows, near_width), wide)] * 3
        + [dma((4, reach * PIECES))] * 2
        + [dma((head_total,))] * 2
        + [dma((classes,))] * 4
        + [dma((reach + 1,))] * 2
        + [pltpu.VMEM((NEAR, (reach + 1) * rows, rows), wide)] * 4,
        compiler_params=pltpu.CompilerParams(collective_id=0, has_side_effects=True),
    )(
        head_kind, raw_queries, raw_keys, values, output_gradient,
        query_gain.reshape(1, width), key_gain.reshape(1, width),
    )


def solution(mesh):
    both = P("ctx", "head")
    placed = (both, both, both, both, P("head"), P("head"), P("head"))
    return jax.shard_map(
        functools.partial(on_device, mesh.shape["ctx"], mesh.shape["head"]),
        mesh=mesh,
        in_specs=placed,
        out_specs=(both, both, both),
        check_vma=False,
    )
```
